256 devices in a mesh: group: 4 (over z_hi), member: 64 (over y, x, z_lo, core).
Axes of the slice: x: 4, y: 4, z: 8 (z_hi: 4, z_lo: 2; z = z_hi * 2 + z_lo), core: 2. Of those that a mesh axis runs over, the one named last changes fastest.
Arguments:
- audio_vectors: bfloat16 [32768, 768], P(('group', 'member')), may hold values from -8 to 8
- sentence_vectors: bfloat16 [16384, 768], P(('group', 'member')), may hold values from -8 to 8
- matching_indices: int32 [32768], P(('group', 'member')), may hold values from 0 to 16383, as said below
- sharpness_array: float32 [1], replicated, may hold values from 8 to 16
- offset_term: float32 [1], replicated, may hold values from -4 to -2
Outputs:
- speech_grad: float32 [32768, 768], P(('group', 'member'))
- text_grad: float32 [16384, 768], P(('group', 'member'))
The draws below stay inside these ranges and needn't reach their ends.
Inputs may be any that keep to these rules, and one draw needn't show every extreme that they name: `matching_indices`: each caption matches exactly two speech clips.
All inputs are finite; a program needn't handle non-finite values.
Results may differ from the reference program's by a relative error of at most 0.00072.
Values may be sent and summed in bfloat16 or wider, within the bound.
A program may use at most 128 MiB of HBM per device.

```python
import math
import jax
import jax.numpy as jnp
from jax import lax

E = 768
BATCH = 32768
CAPTION_TOTAL = 16384


cluster_count = 16


def shared_parts(key):
    centers = jnp.clip(jax.random.normal(jax.random.fold_in(key, 101), (cluster_count, E), jnp.float32), -4.0, 4.0)
    return centers


def tower_rows(key, salt, count):
    centers = shared_parts(key)
    own_key = jax.random.fold_in(key, salt)
    labels = jax.random.randint(jax.random.fold_in(own_key, 1), (count,), 0, cluster_count).astype(jnp.int32)
    picked = centers[labels]
    weight = jnp.exp(jax.random.uniform(jax.random.fold_in(own_key, 2), (count,), jnp.float32, math.log(0.5), math.log(1.8)))
    noise = jnp.clip(jax.random.normal(jax.random.fold_in(own_key, 3), (count, E), jnp.float32), -4.0, 4.0)
    scales = jnp.exp(jax.random.uniform(jax.random.fold_in(own_key, 4), (count,), jnp.float32, 0.0, math.log(10.0)))
    values = weight[:, None] * picked + noise
    return (0.04 * scales[:, None] * values).astype(jnp.bfloat16)


def draw_audio_vectors(key, part):
    return tower_rows(key, 11, BATCH)


def draw_sentence_vectors(key, part):
    return tower_rows(key, 22, CAPTION_TOTAL)


def draw_matching_indices(key, part):
    order = jax.random.permutation(key, BATCH).astype(jnp.int32)
    return (order // 2).astype(jnp.int32)


def setup_inputs(seed: int = 0) -> dict:
    key_of = jax.random.split(jax.random.key(seed), 6)
    return {
        "audio_vectors": draw_audio_vectors(jax.random.fold_in(key_of[5], 71), 0),
        "sentence_vectors": draw_sentence_vectors(jax.random.fold_in(key_of[5], 71), 0),
        "matching_indices": draw_matching_indices(jax.random.fold_in(key_of[5], 71), 0),
        "sharpness_array": jnp.clip(jnp.exp(jax.random.uniform(key_of[3], (1,), jnp.float32, math.log(8.0), math.log(16.0))), 8.0, 16.0),
        "offset_term": jnp.clip(jax.random.uniform(key_of[4], (1,), jnp.float32, -4.0, -2.0), -4.0, -2.0),
    }


def unit_rows(values):
    floats = values.astype(jnp.float32)
    norms = jnp.sqrt(lax.optimization_barrier(jnp.sum(floats * floats, axis=-1, keepdims=True)) + 1e-06)
    return (floats / norms, norms)

def project_gradient(back, direction, norms):
    along = lax.optimization_barrier(jnp.sum(direction * back, axis=-1, keepdims=True))
    return (back - direction * along) / norms

def reference(audio_vectors, sentence_vectors, matching_indices, sharpness_array, offset_term):
    audio_heading, speech_norm = unit_rows(audio_vectors)
    text_dir, text_norm = unit_rows(sentence_vectors)
    speech_unit = audio_heading.astype(jnp.bfloat16)
    text_normalized = text_dir.astype(jnp.bfloat16)
    sharpness_factor = sharpness_array[0]
    shift = offset_term[0]
    block = math.gcd(BATCH, 1024)
    count = BATCH // block
    columns = jnp.arange(CAPTION_TOTAL, dtype=jnp.int32)

    def one_block(text_back, index):
        start = (index * block).astype(jnp.int32)
        rows = lax.dynamic_slice_in_dim(speech_unit, start, block, 0)
        marks = lax.dynamic_slice_in_dim(matching_indices, start, block, 0)
        logits = sharpness_factor * jnp.dot(rows, text_normalized.T, preferred_element_type=jnp.float32) + shift
        match = (marks[:, None] == columns[None, :]).astype(jnp.float32)
        coef = (sharpness_factor * (jax.nn.sigmoid(logits) - match)).astype(jnp.bfloat16)
        speech_part = jnp.dot(coef, text_normalized, preferred_element_type=jnp.float32)
        text_back = text_back + jnp.dot(coef.T, rows, preferred_element_type=jnp.float32)
        return (text_back, speech_part)
    start_back = jnp.zeros((CAPTION_TOTAL, E), jnp.float32)
    text_back, speech_pieces = lax.scan(one_block, start_back, jnp.arange(count, dtype=jnp.int32))
    speech_gradient_back = speech_pieces.reshape(BATCH, E)
    speech_grad = project_gradient(speech_gradient_back, audio_heading, speech_norm)
    text_grad = project_gradient(text_back, text_dir, text_norm)
    return (speech_grad, text_grad)
```

```python
import functools

import jax
import jax.numpy as jnp
from jax import lax
from jax.experimental import pallas as pl
from jax.experimental.pallas import tpu as pltpu
from jax.sharding import Mesh
from jax.sharding import PartitionSpec as P

AXES = ("zh", "y", "x", "zl", "c")
MESH_ID = pl.DeviceIdType.MESH
F32 = jnp.float32
BF16 = jnp.bfloat16

L1, R1, L2, R2, L3, R3, OWN, D4 = range(8)
NR, NT, E = 128, 64, 768
HALF = NR // 2
SLAB = 128
SUB = 32
CHUNK = 512


def unit(values):
    floats = values.astype(F32)
    norms = jnp.sqrt(jnp.sum(floats * floats, axis=-1, keepdims=True) + 1e-06)
    return floats / norms, norms


def project(back, values):
    direction, norms = unit(values)
    along = jnp.sum(direction * back, axis=-1, keepdims=True)
    return (back - direction * along) / norms


def kernel(
    sharp_ref, shift_ref, audio_ref, text_ref, label_ref,
    speech_out, text_out,
    s_all, t_all, labels, ids, t_back, s_back,
    z_from_left, z_from_right, sib_back, slab_low, slab_high, sub_low, sub_high,
    send_sems, recv_sems,
):
    zh, y, x, zl, c = (lax.axis_index(a) for a in AXES)
    z = zh * 2 + zl

    def at_z(step):
        other = (z + step) % 8
        return (other // 2, y, x, other % 2, c)

    def at_y(step):
        return (zh, (y + step) % 4, x, zl, c)

    def at_x(step):
        return (zh, y, (x + step) % 4, zl, c)

    sibling = (zh, y, x, zl, 1 - c)
    copies = {}

    def copy(name, src, dst, device):
        q = len(copies)
        copies[name] = pltpu.make_async_remote_copy(
            src_ref=src, dst_ref=dst, send_sem=send_sems.at[q], recv_sem=recv_sems.at[q],
            device_id=device, device_id_type=MESH_ID,
        )

    def start(*names):
        for name in names:
            copies[name].start()

    def wait(*names):
        for name in names:
            copies[name].wait_recv()

    def s_rows(slot, half=None):
        if half is None:
            return s_all.at[pl.ds(slot * NR, NR)]
        return s_all.at[pl.ds(slot * NR + half * HALF, HALF)]

    def t_base(k, core, which):
        return k * CHUNK + core * 2 * SLAB + which * SLAB

    def t_rows(k, core, which, first, count):
        return t_all.at[pl.ds(t_base(k, core, which) + first, count)]

    def lab(slot):
        return labels.at[pl.ds(slot * 8, 8)]

    up = ((OWN, L1), (L1, L2), (L2, L3))
    down = ((OWN, R1), (R1, R2), (R2, R3))
    for pairs, step in ((up, 1), (down, -1)):
        for src, dst in pairs:
            for half in (0, 1):
                copy(("s", dst, half), s_rows(src, half), s_rows(dst, half), at_z(step))
            copy(("l", dst), lab(src), lab(dst), at_z(step))
    copy(("s", D4, 0), s_rows(L3, 0), s_rows(D4, 0), at_z(1))
    copy(("s", D4, 1), s_rows(R3, 1), s_rows(D4, 1), at_z(-1))
    copy(("l", D4), lab(L3), lab(D4), at_z(1))

    for w, (first, second) in enumerate(((at_x, at_y), (at_y, at_x))):
        piece = lambda j, lo=0, n=SUB: t_rows(0, 0, w, j * SUB + lo, n)
        copy(("t1", w, 1), piece(0), piece(1), first(1))
        copy(("t1", w, 2), piece(0), piece(2), first(-1))
        copy(("t1", w, 3, 0), piece(1, 0, 16), piece(3, 0, 16), first(1))
        copy(("t1", w, 3, 1), piece(2, 16, 16), piece(3, 16, 16), first(-1))
        for j in range(4):
            copy(("t2", w, 1, j), piece(j), t_rows(1, 0, w, j * SUB, SUB), second(1))
            copy(("t2", w, 2, j), piece(j), t_rows(2, 0, w, j * SUB, SUB), second(-1))
        copy(("t2", w, 3, 0), t_rows(1, 0, w, 0, 64), t_rows(3, 0, w, 0, 64), second(1))
        copy(("t2", w, 3, 1), t_rows(2, 0, w, 64, 64), t_rows(3, 0, w, 64, 64), second(-1))
        for k in range(4):
            copy(("ts", w, k), t_rows(k, 0, w, 0, SLAB), t_rows(k, 1, w, 0, SLAB), sibling)

    def sb(slot, half):
        return s_back.at[pl.ds(slot * NR + half * HALF, HALF)]

    def landing(buf, order, half):
        return buf.at[pl.ds((order * 2 + half) * HALF, HALF)]

    for buf, chain, step, d4half in (
        (z_from_left, (D4, R3, R2, R1, OWN), 1, 0), (z_from_right, (D4, L3, L2, L1, OWN), -1, 1)
    ):
        for order, src in enumerate(chain[:-1]):
            for half in (0, 1):
                if src == D4 and half != d4half:
                    continue
                copy(("zr", step, order, half), sb(src, half), landing(buf, order, half), at_z(step))

    def tb(k, which, first, count):
        return t_back.at[pl.ds(t_base(k, 0, which) + first, count)]

    for k in range(4):
        copy(
            ("sr", k), t_back.at[pl.ds(t_base(k, 1, 0), 2 * SLAB)],
            sib_back.at[pl.ds(k * 2 * SLAB, 2 * SLAB)], sibling,
        )
    for w, (first, second) in enumerate(((at_x, at_y), (at_y, at_x))):
        slab_at = lambda buf, order, half: buf.at[pl.ds(w * 256 + order * 128 + half * 64, 64)]
        sub_at = lambda buf, order, half: buf.at[pl.ds(w * 64 + order * 32 + half * 16, 16)]
        for buf, k, step, d2half in ((slab_low, 2, 1, 0), (slab_high, 1, -1, 1)):
            copy(("r2", w, step, 0, d2half), tb(3, w, d2half * 64, 64), slab_at(buf, 0, d2half), second(step))
            for half in (0, 1):
                copy(("r2", w, step, 1, half), tb(k, w, half * 64, 64), slab_at(buf, 1, half), second(step))
        for buf, j, step, d2half in ((sub_low, 2, 1, 0), (sub_high, 1, -1, 1)):
            copy(
                ("r1", w, step, 0, d2half), tb(0, w, 3 * SUB + d2half * 16, 16),
                sub_at(buf, 0, d2half), first(step),
            )
            for half in (0, 1):
                copy(
                    ("r1", w, step, 1, half), tb(0, w, j * SUB + half * 16, 16),
                    sub_at(buf, 1, half), first(step),
                )

    barrier = pltpu.get_barrier_semaphore()
    for device in (at_z(1), at_z(-1), at_y(1), at_y(-1), at_x(1), at_x(-1), sibling):
        pl.semaphore_signal(barrier, inc=1, device_id=device, device_id_type=MESH_ID)

    s_all[pl.ds(OWN * NR, NR), :] = unit(audio_ref[...])[0].astype(BF16)
    t_unit = unit(text_ref[...])[0].astype(BF16)
    t_all[pl.ds(t_base(0, 0, 0), SUB), :] = t_unit[:SUB]
    t_all[pl.ds(t_base(0, 0, 1), SUB), :] = t_unit[SUB:]
    labels[pl.ds(OWN * 8, 8), :] = jnp.broadcast_to(label_ref[...], (8, NR))

    row = lax.broadcasted_iota(jnp.int32, ids.shape, 0)
    k, core, which, j, r = row >> 9, (row >> 8) & 1, (row >> 7) & 1, (row >> 5) & 3, row & 31

    def shift_of(slot):
        return jnp.where(slot == 1, 3, jnp.where(slot == 2, 1, jnp.where(slot == 3, 2, 0)))

    dk, dj = shift_of(k), shift_of(j)
    row_y = (y + jnp.where(which == 0, dk, dj)) & 3
    row_x = (x + jnp.where(which == 0, dj, dk)) & 3
    row_c = c ^ core
    ids[...] = zh * 4096 + row_y * 1024 + row_x * 256 + zl * 128 + row_c * 64 + which * 32 + r

    pl.semaphore_wait(barrier, 7)

    start(("l", L1), ("l", R1), ("t1", 0, 1), ("t1", 0, 2), ("t1", 1, 1), ("t1", 1, 2))
    start(("s", L1, 0), ("s", R1, 1), ("s", L1, 1), ("s", R1, 0))
    for w in (0, 1):
        start(("t2", w, 1, 0), ("t2", w, 2, 0))
    t_back[...] = jnp.zeros_like(t_back)
    s_back[...] = jnp.zeros_like(s_back)
    for w in (0, 1):
        wait(("t1", w, 1))
        start(("t1", w, 3, 0), ("t2", w, 1, 1), ("t2", w, 2, 1))
        wait(("t1", w, 2))
        start(("t1", w, 3, 1), ("t2", w, 1, 2), ("t2", w, 2, 2))
    wait(("l", L1), ("l", R1))
    start(("l", L2), ("l", R2))
    wait(("s", L1, 0), ("s", R1, 1))
    start(("s", L2, 0), ("s", R2, 1))
    for w in (0, 1):
        wait(("t1", w, 3, 0), ("t1", w, 3, 1))
        start(("t2", w, 1, 3), ("t2", w, 2, 3), ("ts", w, 0))
    wait(("s", L1, 1), ("s", R1, 0))
    start(("s", L2, 1), ("s", R2, 0))
    for w in (0, 1):
        wait(("t2", w, 1, 0), ("t2", w, 1, 1))
        start(("t2", w, 3, 0))
        wait(("t2", w, 2, 2), ("t2", w, 2, 3))
        start(("t2", w, 3, 1))
    wait(("ts", 0, 0), ("ts", 1, 0))

    def before_1():
        for w in (0, 1):
            wait(("t2", w, 1, 2), ("t2", w, 1, 3))
            start(("ts", w, 1))
            wait(("t2", w, 2, 0), ("t2", w, 2, 1))
            start(("ts", w, 2))
        wait(("l", L2), ("l", R2))
        start(("l", L3), ("l", R3))
        wait(("s", L2, 0), ("s", R2, 1))
        start(("s", L3, 0), ("s", R3, 1))
        wait(("ts", 0, 1), ("ts", 1, 1))

    def before_2():
        wait(("ts", 0, 2), ("ts", 1, 2))
        for w in (0, 1):
            wait(("t2", w, 3, 0), ("t2", w, 3, 1))
            start(("ts", w, 3))

    def before_3():
        wait(("ts", 0, 3), ("ts", 1, 3))
        wait(("s", L2, 1), ("s", R2, 0))
        start(("s", L3, 1), ("s", R3, 0))

    def before_5():
        wait(("l", L3), ("l", R3))
        start(("l", D4))
        wait(("s", L3, 0), ("s", R3, 1))
        start(("s", D4, 0), ("s", D4, 1))

    def before_8():
        wait(("s", L3, 1), ("s", R3, 0))

    def before_12():
        wait(("s", D4, 0), ("s", D4, 1), ("l", D4))

    before = {1: before_1, 2: before_2, 3: before_3, 5: before_5, 8: before_8, 12: before_12}
    last_order = (3, 1, 2, 0)

    sharp = sharp_ref[0]
    shift = shift_ref[0]

    def one_chunk(i, carry):
        for when, act in before.items():
            pl.when(i == when)(act)
        u = i // 4
        n = i % 4
        k = jnp.where(u == 3, jnp.where(n == 0, 3, jnp.where(n == 3, 0, n)), n)
        first = pl.multiple_of(u * 256, 256)
        speech = s_all[pl.ds(first, 256), :]
        lab_pair = labels[pl.ds(pl.multiple_of(u * 16, 16), 16), :]
        part = jnp.zeros((256, E), F32)
        for half in range(2):
            rows = pl.ds(pl.multiple_of(k * CHUNK + half * 256, 256), 256)
            text = t_all[rows, :]
            logits = lax.dot_general(text, speech, (((1,), (1,)), ((), ())), preferred_element_type=F32)
            logits = sharp * logits + shift
            number = ids[rows, :]
            match = jnp.concatenate([number == lab_pair[0:1, :], number == lab_pair[8:9, :]], axis=1)
            coef = sharp * (1.0 / (1.0 + jnp.exp(-logits)) - match.astype(F32))
            coef = coef.astype(BF16)
            t_back[rows, :] += jnp.dot(coef, speech, preferred_element_type=F32)
            part += lax.dot_general(coef, text, (((0,), (0,)), ((), ())), preferred_element_type=F32)
        s_back[pl.ds(first, 256), :] += part
        for m, which_k in enumerate(last_order):
            pl.when(i == 12 + m)(functools.partial(start, ("sr", which_k)))
        return carry

    lax.fori_loop(0, 16, one_chunk, 0)

    def add(ref, other):
        ref[...] += other[...]

    start(("zr", 1, 0, 0), ("zr", -1, 0, 1), ("zr", 1, 1, 1), ("zr", -1, 1, 0))

    def merge_sibling(k):
        wait(("sr", k))
        add(t_back.at[pl.ds(t_base(k, 0, 0), 2 * SLAB)], sib_back.at[pl.ds(k * 2 * SLAB, 2 * SLAB)])

    merge_sibling(3)
    for w in (0, 1):
        start(("r2", w, 1, 0, 0), ("r2", w, -1, 0, 1))
    merge_sibling(2)
    for w in (0, 1):
        start(("r2", w, 1, 1, 1))
    merge_sibling(1)
    for w in (0, 1):
        start(("r2", w, -1, 1, 0))

    def z_step(order, half):
        for buf, chain, step in (
            (z_from_left, (D4, R3, R2, R1, OWN), 1), (z_from_right, (D4, L3, L2, L1, OWN), -1)
        ):
            h = half if step == 1 else 1 - half
            wait(("zr", step, order, h))
            add(sb(chain[order + 1], h), landing(buf, order, h))
            if order < 3:
                start(("zr", step, order + 1, h))

    for w in (0, 1):
        slab_at = lambda buf, order, half: buf.at[pl.ds(w * 256 + order * 128 + half * 64, 64)]
        wait(("r2", w, 1, 0, 0))
        add(tb(2, w, 0, 64), slab_at(slab_low, 0, 0))
        start(("r2", w, 1, 1, 0))
        wait(("r2", w, -1, 0, 1))
        add(tb(1, w, 64, 64), slab_at(slab_high, 0, 1))
        start(("r2", w, -1, 1, 1))
    merge_sibling(0)
    z_step(0, 0)
    z_step(1, 1)
    for w in (0, 1):
        slab_at = lambda buf, order, half: buf.at[pl.ds(w * 256 + order * 128 + half * 64, 64)]
        for half in (1, 0):
            wait(("r2", w, 1, 1, half), ("r2", w, -1, 1, half))
            ref = tb(0, w, half * 64, 64)
            ref[...] += slab_at(slab_low, 1, half)[...] + slab_at(slab_high, 1, half)[...]
        start(("r1", w, 1, 0, 0), ("r1", w, -1, 0, 1), ("r1", w, 1, 1, 1), ("r1", w, -1, 1, 0))
    z_step(1, 0)
    for w in (0, 1):
        sub_at = lambda buf, order, half: buf.at[pl.ds(w * 64 + order * 32 + half * 16, 16)]
        wait(("r1", w, 1, 0, 0))
        add(tb(0, w, 2 * SUB, 16), sub_at(sub_low, 0, 0))
        start(("r1", w, 1, 1, 0))
        wait(("r1", w, -1, 0, 1))
        add(tb(0, w, SUB + 16, 16), sub_at(sub_high, 0, 1))
        start(("r1", w, -1, 1, 1))
    z_step(2, 1)
    z_step(2, 0)
    for w in (0, 1):
        rows = pl.ds(w * SUB, SUB)
        for half in (0, 1):
            wait(("r1", w, 1, 1, half), ("r1", w, -1, 1, half))
        landed = pl.ds(w * 64 + 32, 32)
        back = tb(0, w, 0, SUB)[...] + sub_low[landed, :] + sub_high[landed, :]
        text_out[rows, :] = project(back, text_ref[rows, :])
    z_step(3, 1)
    z_step(3, 0)
    speech_out[...] = project(s_back[pl.ds(OWN * NR, NR), :], audio_ref[...])

    for done in copies.values():
        done.wait_send()
    assert len(copies) == COPIES


COPIES = 14 + 7 + 2 * (4 + 8 + 2 + 4) + 14 + 4 + 2 * 12


def shards(audio, sentence, matching, sharpness, offset):
    vmem = pl.BlockSpec(memory_space=pltpu.VMEM)
    smem = pl.BlockSpec(memory_space=pltpu.SMEM)
    return pl.pallas_call(
        kernel,
        out_shape=(jax.ShapeDtypeStruct((NR, E), F32), jax.ShapeDtypeStruct((NT, E), F32)),
        in_specs=[smem, smem, vmem, vmem, vmem],
        out_specs=(vmem, vmem),
        scratch_shapes=[
            pltpu.VMEM((8 * NR, E), BF16),
            pltpu.VMEM((4 * CHUNK, E), BF16),
            pltpu.VMEM((64, NR), jnp.int32),
            pltpu.VMEM((4 * CHUNK, 128), jnp.int32),
            pltpu.VMEM((4 * CHUNK, E), F32),
            pltpu.VMEM((8 * NR, E), F32),
            pltpu.VMEM((4 * NR, E), F32),
            pltpu.VMEM((4 * NR, E), F32),
            pltpu.VMEM((2 * CHUNK, E), F32),
            pltpu.VMEM((512, E), F32),
            pltpu.VMEM((512, E), F32),
            pltpu.VMEM((128, E), F32),
            pltpu.VMEM((128, E), F32),
            pltpu.SemaphoreType.DMA((COPIES,)),
            pltpu.SemaphoreType.DMA((COPIES,)),
        ],
        compiler_params=pltpu.CompilerParams(
            collective_id=0, has_side_effects=True, vmem_limit_bytes=60 * 1024 * 1024
        ),
    )(sharpness, offset, audio, sentence, matching.reshape(1, NR))


def solution(mesh):
    split = Mesh(mesh.devices.reshape(4, 4, 4, 2, 2), AXES)
    rows = P(AXES)
    return jax.shard_map(
        shards,
        mesh=split,
        in_specs=(rows, rows, rows, P(), P()),
        out_specs=(rows, rows),
        check_vma=False,
    )
```

```python
import functools

import jax
import jax.numpy as jnp
from jax import lax
from jax.experimental import pallas as pl
from jax.experimental.pallas import tpu as pltpu
from jax.sharding import Mesh
from jax.sharding import PartitionSpec as P

AXES = ("zh", "y", "x", "zl", "c")
MESH_ID = pl.DeviceIdType.MESH
F32 = jnp.float32
BF16 = jnp.bfloat16

L1, R1, L2, R2, L3, R3, OWN, D4 = range(8)
NR, NT, E = 128, 64, 768
HALF = NR // 2
SLAB = 128
SUB = 32
CHUNK = 512


def unit(values):
    floats = values.astype(F32)
    norms = jnp.sqrt(jnp.sum(floats * floats, axis=-1, keepdims=True) + 1e-06)
    return floats / norms, norms


def project(back, values):
    direction, norms = unit(values)
    along = jnp.sum(direction * back, axis=-1, keepdims=True)
    return (back - direction * along) / norms


def kernel(
    sharp_ref, shift_ref, audio_ref, text_ref, label_ref,
    speech_out, text_out,
    s_all, t_all, labels, ids, t_back, s_back,
    z_from_left, z_from_right, sib_back, slab_low, slab_high, sub_low, sub_high,
    coef_even, coef_odd, send_sems, recv_sems,
):
    zh, y, x, zl, c = (lax.axis_index(a) for a in AXES)
    z = zh * 2 + zl

    def at_z(step):
        other = (z + step) % 8
        return (other // 2, y, x, other % 2, c)

    def at_y(step):
        return (zh, (y + step) % 4, x, zl, c)

    def at_x(step):
        return (zh, y, (x + step) % 4, zl, c)

    sibling = (zh, y, x, zl, 1 - c)
    copies = {}

    def copy(name, src, dst, device):
        q = len(copies)
        copies[name] = pltpu.make_async_remote_copy(
            src_ref=src, dst_ref=dst, send_sem=send_sems.at[q], recv_sem=recv_sems.at[q],
            device_id=device, device_id_type=MESH_ID,
        )

    def start(*names):
        for name in names:
            copies[name].start()

    def wait(*names):
        for name in names:
            copies[name].wait_recv()

    def s_rows(slot, half=None):
        if half is None:
            return s_all.at[pl.ds(slot * NR, NR)]
        return s_all.at[pl.ds(slot * NR + half * HALF, HALF)]

    def t_base(k, core, which):
        return k * CHUNK + core * 2 * SLAB + which * SLAB

    def t_rows(k, core, which, first, count):
        return t_all.at[pl.ds(t_base(k, core, which) + first, count)]

    def lab(slot):
        return labels.at[pl.ds(slot * 8, 8)]

    up = ((OWN, L1), (L1, L2), (L2, L3))
    down = ((OWN, R1), (R1, R2), (R2, R3))
    for pairs, step in ((up, 1), (down, -1)):
        for src, dst in pairs:
            for half in (0, 1):
                copy(("s", dst, half), s_rows(src, half), s_rows(dst, half), at_z(step))
            copy(("l", dst), lab(src), lab(dst), at_z(step))
    copy(("s", D4, 0), s_rows(L3, 0), s_rows(D4, 0), at_z(1))
    copy(("s", D4, 1), s_rows(R3, 1), s_rows(D4, 1), at_z(-1))
    copy(("l", D4), lab(L3), lab(D4), at_z(1))

    for w, (first, second) in enumerate(((at_x, at_y), (at_y, at_x))):
        piece = lambda j, lo=0, n=SUB: t_rows(0, 0, w, j * SUB + lo, n)
        copy(("t1", w, 1), piece(0), piece(1), first(1))
        copy(("t1", w, 2), piece(0), piece(2), first(-1))
        copy(("t1", w, 3, 0), piece(1, 0, 16), piece(3, 0, 16), first(1))
        copy(("t1", w, 3, 1), piece(2, 16, 16), piece(3, 16, 16), first(-1))
        for j in range(4):
            copy(("t2", w, 1, j), piece(j), t_rows(1, 0, w, j * SUB, SUB), second(1))
            copy(("t2", w, 2, j), piece(j), t_rows(2, 0, w, j * SUB, SUB), second(-1))
        copy(("t2", w, 3, 0), t_rows(1, 0, w, 0, 64), t_rows(3, 0, w, 0, 64), second(1))
        copy(("t2", w, 3, 1), t_rows(2, 0, w, 64, 64), t_rows(3, 0, w, 64, 64), second(-1))
        for k in range(4):
            copy(("ts", w, k), t_rows(k, 0, w, 0, SLAB), t_rows(k, 1, w, 0, SLAB), sibling)

    def sb(slot, half):
        return s_back.at[pl.ds(slot * NR + half * HALF, HALF)]

    def landing(buf, order, half):
        return buf.at[pl.ds((order * 2 + half) * HALF, HALF)]

    for buf, chain, step, d4half in (
        (z_from_left, (D4, R3, R2, R1, OWN), 1, 0), (z_from_right, (D4, L3, L2, L1, OWN), -1, 1)
    ):
        for order, src in enumerate(chain[:-1]):
            for half in (0, 1):
                if src == D4 and half != d4half:
                    continue
                copy(("zr", step, order, half), sb(src, half), landing(buf, order, half), at_z(step))

    def tb(k, which, first, count):
        return t_back.at[pl.ds(t_base(k, 0, which) + first, count)]

    for k in range(4):
        copy(
            ("sr", k), t_back.at[pl.ds(t_base(k, 1, 0), 2 * SLAB)],
            sib_back.at[pl.ds(k * 2 * SLAB, 2 * SLAB)], sibling,
        )
    for w, (first, second) in enumerate(((at_x, at_y), (at_y, at_x))):
        slab_at = lambda buf, order, half: buf.at[pl.ds(w * 256 + order * 128 + half * 64, 64)]
        sub_at = lambda buf, order, half: buf.at[pl.ds(w * 64 + order * 32 + half * 16, 16)]
        for buf, k, step, d2half in ((slab_low, 2, 1, 0), (slab_high, 1, -1, 1)):
            copy(("r2", w, step, 0, d2half), tb(3, w, d2half * 64, 64), slab_at(buf, 0, d2half), second(step))
            for half in (0, 1):
                copy(("r2", w, step, 1, half), tb(k, w, half * 64, 64), slab_at(buf, 1, half), second(step))
        for buf, j, step, d2half in ((sub_low, 2, 1, 0), (sub_high, 1, -1, 1)):
            copy(
                ("r1", w, step, 0, d2half), tb(0, w, 3 * SUB + d2half * 16, 16),
                sub_at(buf, 0, d2half), first(step),
            )
            for half in (0, 1):
                copy(
                    ("r1", w, step, 1, half), tb(0, w, j * SUB + half * 16, 16),
                    sub_at(buf, 1, half), first(step),
                )

    barrier = pltpu.get_barrier_semaphore()
    for device in (at_z(1), at_z(-1), at_y(1), at_y(-1), at_x(1), at_x(-1), sibling):
        pl.semaphore_signal(barrier, inc=1, device_id=device, device_id_type=MESH_ID)

    s_all[pl.ds(OWN * NR, NR), :] = unit(audio_ref[...])[0].astype(BF16)
    t_unit = unit(text_ref[...])[0].astype(BF16)
    t_all[pl.ds(t_base(0, 0, 0), SUB), :] = t_unit[:SUB]
    t_all[pl.ds(t_base(0, 0, 1), SUB), :] = t_unit[SUB:]
    labels[pl.ds(OWN * 8, 8), :] = jnp.broadcast_to(label_ref[...], (8, NR))

    row = lax.broadcasted_iota(jnp.int32, ids.shape, 0)
    k, core, which, j, r = row >> 9, (row >> 8) & 1, (row >> 7) & 1, (row >> 5) & 3, row & 31

    def shift_of(slot):
        return jnp.where(slot == 1, 3, jnp.where(slot == 2, 1, jnp.where(slot == 3, 2, 0)))

    dk, dj = shift_of(k), shift_of(j)
    row_y = (y + jnp.where(which == 0, dk, dj)) & 3
    row_x = (x + jnp.where(which == 0, dj, dk)) & 3
    row_c = c ^ core
    ids[...] = zh * 4096 + row_y * 1024 + row_x * 256 + zl * 128 + row_c * 64 + which * 32 + r

    pl.semaphore_wait(barrier, 7)

    start(("l", L1), ("l", R1), ("t1", 0, 1), ("t1", 0, 2), ("t1", 1, 1), ("t1", 1, 2))
    start(("s", L1, 0), ("s", R1, 1), ("s", L1, 1), ("s", R1, 0))
    for w in (0, 1):
        start(("t2", w, 1, 0), ("t2", w, 2, 0))
    t_back[...] = jnp.zeros_like(t_back)
    s_back[...] = jnp.zeros_like(s_back)
    for w in (0, 1):
        wait(("t1", w, 1))
        start(("t1", w, 3, 0), ("t2", w, 1, 1), ("t2", w, 2, 1))
        wait(("t1", w, 2))
        start(("t1", w, 3, 1), ("t2", w, 1, 2), ("t2", w, 2, 2))
    wait(("l", L1), ("l", R1))
    start(("l", L2), ("l", R2))
    wait(("s", L1, 0), ("s", R1, 1))
    start(("s", L2, 0), ("s", R2, 1))
    for w in (0, 1):
        wait(("t1", w, 3, 0), ("t1", w, 3, 1))
        start(("t2", w, 1, 3), ("t2", w, 2, 3), ("ts", w, 0))
    wait(("s", L1, 1), ("s", R1, 0))
    start(("s", L2, 1), ("s", R2, 0))
    for w in (0, 1):
        wait(("t2", w, 1, 0), ("t2", w, 1, 1))
        start(("t2", w, 3, 0))
        wait(("t2", w, 2, 2), ("t2", w, 2, 3))
        start(("t2", w, 3, 1))
    wait(("ts", 0, 0), ("ts", 1, 0))

    def before_0():
        for w in (0, 1):
            wait(("t2", w, 1, 2), ("t2", w, 1, 3))
            start(("ts", w, 1))
            wait(("t2", w, 2, 0), ("t2", w, 2, 1))
            start(("ts", w, 2))
        wait(("ts", 0, 1), ("ts", 1, 1))

    def before_1():
        wait(("ts", 0, 2), ("ts", 1, 2))
        wait(("l", L2), ("l", R2))
        start(("l", L3), ("l", R3))
        wait(("s", L2, 0), ("s", R2, 1))
        start(("s", L3, 0), ("s", R3, 1))
        for w in (0, 1):
            wait(("t2", w, 3, 0), ("t2", w, 3, 1))
            start(("ts", w, 3))

    def before_2():
        wait(("ts", 0, 3), ("ts", 1, 3))

    def before_3():
        wait(("s", L2, 1), ("s", R2, 0))
        start(("s", L3, 1), ("s", R3, 0))

    def before_5():
        wait(("l", L3), ("l", R3))
        start(("l", D4))
        wait(("s", L3, 0), ("s", R3, 1))
        start(("s", D4, 0), ("s", D4, 1))

    def before_7():
        wait(("s", L3, 1), ("s", R3, 0))

    def before_11():
        wait(("s", D4, 0), ("s", D4, 1), ("l", D4))

    def before_12():
        start(("zr", 1, 1, 1), ("zr", -1, 1, 0))

    def before_13():
        start(("sr", 3))

    before = {
        0: before_0, 1: before_1, 2: before_2, 3: before_3, 5: before_5, 7: before_7, 11: before_11,
        12: before_12, 13: before_13,
    }

    sharp = sharp_ref[0]
    shift = shift_ref[0]

    def place(i):
        u = i // 4
        n = i % 4
        k = jnp.where(u == 3, jnp.where(n == 0, 3, jnp.where(n == 3, 0, n)), n)
        return pl.multiple_of(u * 256, 256), pl.multiple_of(k * CHUNK, CHUNK), pl.multiple_of(u * 16, 16)

    def forward(i, coefs):
        s0, t0, l0 = place(i)
        speech = s_all[pl.ds(s0, 256), :]
        lab_pair = labels[pl.ds(l0, 16), :]
        for half in range(2):
            rows = pl.ds(pl.multiple_of(t0 + half * 256, 256), 256)
            logits = lax.dot_general(
                t_all[rows, :], speech, (((1,), (1,)), ((), ())), preferred_element_type=F32
            )
            logits = sharp * logits + shift
            number = ids[rows, :]
            match = jnp.concatenate([number == lab_pair[0:1, :], number == lab_pair[8:9, :]], axis=1)
            coef = sharp * (1.0 / (1.0 + jnp.exp(-logits)) - match.astype(F32))
            coefs[pl.ds(half * 256, 256), :] = coef.astype(BF16)

    def backward(i, coefs):
        s0, t0, _ = place(i)
        coef = coefs[...]
        rows = pl.ds(t0, CHUNK)
        s_back[pl.ds(s0, 256), :] += lax.dot_general(
            coef, t_all[rows, :], (((0,), (0,)), ((), ())), preferred_element_type=F32
        )
        t_back[rows, :] += jnp.dot(coef, s_all[pl.ds(s0, 256), :], preferred_element_type=F32)

    forward(0, coef_even)

    def two_chunks(h, carry):
        for parity, ready, filled in ((0, coef_even, coef_odd), (1, coef_odd, coef_even)):
            for when, act in before.items():
                if when % 2 == parity:
                    pl.when(h == when // 2)(act)
            i = h * 2 + parity
            forward(i + 1, filled)
            backward(i, ready)
        return carry

    lax.fori_loop(0, 7, two_chunks, 0)

    def add(ref, other):
        ref[...] += other[...]

    def merge_sibling(k):
        wait(("sr", k))
        add(t_back.at[pl.ds(t_base(k, 0, 0), 2 * SLAB)], sib_back.at[pl.ds(k * 2 * SLAB, 2 * SLAB)])

    start(("sr", 1))
    forward(15, coef_odd)
    backward(14, coef_even)
    start(("sr", 2))
    merge_sibling(3)
    for w in (0, 1):
        start(("r2", w, 1, 0, 0), ("r2", w, -1, 0, 1))
    merge_sibling(1)
    for w in (0, 1):
        start(("r2", w, -1, 1, 0))
    backward(15, coef_odd)
    start(("sr", 0))

    start(("zr", 1, 0, 0), ("zr", -1, 0, 1))
    merge_sibling(2)
    for w in (0, 1):
        start(("r2", w, 1, 1, 1))

    def z_step(order, half):
        for buf, chain, step in (
            (z_from_left, (D4, R3, R2, R1, OWN), 1), (z_from_right, (D4, L3, L2, L1, OWN), -1)
        ):
            h = half if step == 1 else 1 - half
            wait(("zr", step, order, h))
            add(sb(chain[order + 1], h), landing(buf, order, h))
            if order < 3:
                start(("zr", step, order + 1, h))

    for w in (0, 1):
        slab_at = lambda buf, order, half: buf.at[pl.ds(w * 256 + order * 128 + half * 64, 64)]
        wait(("r2", w, 1, 0, 0))
        add(tb(2, w, 0, 64), slab_at(slab_low, 0, 0))
        start(("r2", w, 1, 1, 0))
        wait(("r2", w, -1, 0, 1))
        add(tb(1, w, 64, 64), slab_at(slab_high, 0, 1))
        start(("r2", w, -1, 1, 1))
    merge_sibling(0)
    z_step(0, 0)
    z_step(1, 1)
    for w in (0, 1):
        slab_at = lambda buf, order, half: buf.at[pl.ds(w * 256 + order * 128 + half * 64, 64)]
        for half in (1, 0):
            wait(("r2", w, 1, 1, half), ("r2", w, -1, 1, half))
            ref = tb(0, w, half * 64, 64)
            ref[...] += slab_at(slab_low, 1, half)[...] + slab_at(slab_high, 1, half)[...]
        start(("r1", w, 1, 0, 0), ("r1", w, -1, 0, 1), ("r1", w, 1, 1, 1), ("r1", w, -1, 1, 0))
    z_step(1, 0)
    for w in (0, 1):
        sub_at = lambda buf, order, half: buf.at[pl.ds(w * 64 + order * 32 + half * 16, 16)]
        wait(("r1", w, 1, 0, 0))
        add(tb(0, w, 2 * SUB, 16), sub_at(sub_low, 0, 0))
        start(("r1", w, 1, 1, 0))
        wait(("r1", w, -1, 0, 1))
        add(tb(0, w, SUB + 16, 16), sub_at(sub_high, 0, 1))
        start(("r1", w, -1, 1, 1))
    z_step(2, 1)
    z_step(2, 0)
    for w in (0, 1):
        rows = pl.ds(w * SUB, SUB)
        for half in (0, 1):
            wait(("r1", w, 1, 1, half), ("r1", w, -1, 1, half))
        landed = pl.ds(w * 64 + 32, 32)
        back = tb(0, w, 0, SUB)[...] + sub_low[landed, :] + sub_high[landed, :]
        text_out[rows, :] = project(back, text_ref[rows, :])
    z_step(3, 1)
    z_step(3, 0)
    speech_out[...] = project(s_back[pl.ds(OWN * NR, NR), :], audio_ref[...])

    for done in copies.values():
        done.wait_send()
    assert len(copies) == COPIES


COPIES = 14 + 7 + 2 * (4 + 8 + 2 + 4) + 14 + 4 + 2 * 12


def shards(audio, sentence, matching, sharpness, offset):
    vmem = pl.BlockSpec(memory_space=pltpu.VMEM)
    smem = pl.BlockSpec(memory_space=pltpu.SMEM)
    return pl.pallas_call(
        kernel,
        out_shape=(jax.ShapeDtypeStruct((NR, E), F32), jax.ShapeDtypeStruct((NT, E), F32)),
        in_specs=[smem, smem, vmem, vmem, vmem],
        out_specs=(vmem, vmem),
        scratch_shapes=[
            pltpu.VMEM((8 * NR, E), BF16),
            pltpu.VMEM((4 * CHUNK, E), BF16),
            pltpu.VMEM((64, NR), jnp.int32),
            pltpu.VMEM((4 * CHUNK, 128), jnp.int32),
            pltpu.VMEM((4 * CHUNK, E), F32),
            pltpu.VMEM((8 * NR, E), F32),
            pltpu.VMEM((4 * NR, E), F32),
            pltpu.VMEM((4 * NR, E), F32),
            pltpu.VMEM((2 * CHUNK, E), F32),
            pltpu.VMEM((512, E), F32),
            pltpu.VMEM((512, E), F32),
            pltpu.VMEM((128, E), F32),
            pltpu.VMEM((128, E), F32),
            pltpu.VMEM((CHUNK, 256), BF16),
            pltpu.VMEM((CHUNK, 256), BF16),
            pltpu.SemaphoreType.DMA((COPIES,)),
            pltpu.SemaphoreType.DMA((COPIES,)),
        ],
        compiler_params=pltpu.CompilerParams(
            collective_id=0, has_side_effects=True, vmem_limit_bytes=60 * 1024 * 1024
        ),
    )(sharpness, offset, audio, sentence, matching.reshape(1, NR))


def solution(mesh):
    split = Mesh(mesh.devices.reshape(4, 4, 4, 2, 2), AXES)
    rows = P(AXES)
    return jax.shard_map(
        shards,
        mesh=split,
        in_specs=(rows, rows, rows, P(), P()),
        out_specs=(rows, rows),
        check_vma=False,
    )
```

```python
import functools

import jax
import jax.numpy as jnp
from jax import lax
from jax.experimental import pallas as pl
from jax.experimental.pallas import tpu as pltpu
from jax.sharding import Mesh
from jax.sharding import PartitionSpec as P

AXES = ("zh", "y", "x", "zl", "c")
MESH_ID = pl.DeviceIdType.MESH
F32 = jnp.float32
BF16 = jnp.bfloat16

L1, R1, L2, R2, L3, R3, OWN, D4 = range(8)
NR, NT, E = 128, 64, 768
HALF = NR // 2
PIECE = NR // 4
SLAB = 128
SUB = 32
CHUNK = 512


def unit(values):
    floats = values.astype(F32)
    norms = jnp.sqrt(jnp.sum(floats * floats, axis=-1, keepdims=True) + 1e-06)
    return floats / norms, norms


def project(back, values):
    direction, norms = unit(values)
    along = jnp.sum(direction * back, axis=-1, keepdims=True)
    return (back - direction * along) / norms


def kernel(
    sharp_ref, shift_ref, audio_ref, text_ref, label_ref,
    speech_out, text_out,
    s_all, t_all, labels, ids, t_back, s_back,
    sib_back, q_out, q_in, scale_out, scale_in,
    coef_even, coef_odd, send_sems, recv_sems,
):
    zh, y, x, zl, c = (lax.axis_index(a) for a in AXES)
    z = zh * 2 + zl

    def at_z(step):
        other = (z + step) % 8
        return (other // 2, y, x, other % 2, c)

    def at_y(step):
        return (zh, (y + step) % 4, x, zl, c)

    def at_x(step):
        return (zh, y, (x + step) % 4, zl, c)

    sibling = (zh, y, x, zl, 1 - c)
    copies = {}

    def copy(name, src, dst, device):
        q = len(copies)
        copies[name] = pltpu.make_async_remote_copy(
            src_ref=src, dst_ref=dst, send_sem=send_sems.at[q], recv_sem=recv_sems.at[q],
            device_id=device, device_id_type=MESH_ID,
        )

    def start(*names):
        for name in names:
            copies[name].start()

    def wait(*names):
        for name in names:
            copies[name].wait_recv()

    def s_rows(slot, half=None):
        if half is None:
            return s_all.at[pl.ds(slot * NR, NR)]
        return s_all.at[pl.ds(slot * NR + half * HALF, HALF)]

    def t_base(k, core, which):
        return k * CHUNK + core * 2 * SLAB + which * SLAB

    def t_rows(k, core, which, first, count):
        return t_all.at[pl.ds(t_base(k, core, which) + first, count)]

    def lab(slot):
        return labels.at[pl.ds(slot * 8, 8)]

    up = ((OWN, L1), (L1, L2), (L2, L3))
    down = ((OWN, R1), (R1, R2), (R2, R3))
    for pairs, step in ((up, 1), (down, -1)):
        for src, dst in pairs:
            for half in (0, 1):
                copy(("s", dst, half), s_rows(src, half), s_rows(dst, half), at_z(step))
            copy(("l", dst), lab(src), lab(dst), at_z(step))
    copy(("s", D4, 0), s_rows(L3, 0), s_rows(D4, 0), at_z(1))
    copy(("s", D4, 1), s_rows(R3, 1), s_rows(D4, 1), at_z(-1))
    copy(("l", D4), lab(L3), lab(D4), at_z(1))

    for w, (first, second) in enumerate(((at_x, at_y), (at_y, at_x))):
        piece = lambda j, lo=0, n=SUB: t_rows(0, 0, w, j * SUB + lo, n)
        copy(("t1", w, 1), piece(0), piece(1), first(1))
        copy(("t1", w, 2), piece(0), piece(2), first(-1))
        copy(("t1", w, 3, 0), piece(1, 0, 16), piece(3, 0, 16), first(1))
        copy(("t1", w, 3, 1), piece(2, 16, 16), piece(3, 16, 16), first(-1))
        for j in range(4):
            copy(("t2", w, 1, j), piece(j), t_rows(1, 0, w, j * SUB, SUB), second(1))
            copy(("t2", w, 2, j), piece(j), t_rows(2, 0, w, j * SUB, SUB), second(-1))
        copy(("t2", w, 3, 0), t_rows(1, 0, w, 0, 64), t_rows(3, 0, w, 0, 64), second(1))
        copy(("t2", w, 3, 1), t_rows(2, 0, w, 64, 64), t_rows(3, 0, w, 64, 64), second(-1))
        for k in range(4):
            copy(("ts", w, k), t_rows(k, 0, w, 0, SLAB), t_rows(k, 1, w, 0, SLAB), sibling)

    routes = {}
    used = [0]

    def route(name, ref, rows, device):
        first, n = used[0], len(routes)
        used[0] += rows
        into = (q_in.at[pl.ds(first, rows)], scale_in.at[pl.ds(n * 8, 8)])
        out = (q_out.at[pl.ds(first, rows)], scale_out.at[pl.ds(n * 8, 8)])
        routes[name] = (ref, rows, out, into)
        for what, src, dst in zip("sq", reversed(out), reversed(into)):
            copy((*name, what), src, dst, device)

    def ship(*names):
        for name in names:
            ref, rows, (numbers, scales), _ = routes[name]
            value = ref[...]
            top = jnp.maximum(jnp.max(jnp.abs(value), axis=1, keepdims=True), 1e-30)
            numbers[...] = jnp.round(value * (32767.0 / top)).astype(jnp.int16)
            scale = top * (1.0 / 32767.0)
            lane = lax.broadcasted_iota(jnp.int32, (8, 128), 1)
            tile = jnp.zeros((8, 128), F32)
            for v in range(rows // 8):
                tile = jnp.where(lane == v, scale[v * 8 : v * 8 + 8], tile)
            scales[...] = tile
            start((*name, "s"), (*name, "q"))

    def landed(name):
        _, rows, _, (numbers, scales) = routes[name]
        wait((*name, "s"), (*name, "q"))
        tile = scales[...]
        scale = jnp.concatenate([tile[:, v : v + 1] for v in range(rows // 8)], axis=0)
        return numbers[...].astype(F32) * scale

    def sb(slot, piece):
        return s_back.at[pl.ds(slot * NR + piece * PIECE, PIECE)]

    chains = {1: (D4, R3, R2, R1, OWN), -1: (D4, L3, L2, L1, OWN)}
    far_pieces = {1: (0, 1), -1: (2, 3)}
    for step, chain in chains.items():
        for order, src in enumerate(chain[:-1]):
            for piece in range(4):
                if src != D4 or piece in far_pieces[step]:
                    route(("zr", step, order, piece), sb(src, piece), PIECE, at_z(step))

    def tb(k, which, first, count):
        return t_back.at[pl.ds(t_base(k, 0, which) + first, count)]

    for k in range(4):
        copy(
            ("sr", k), t_back.at[pl.ds(t_base(k, 1, 0), 2 * SLAB)],
            sib_back.at[pl.ds(k * 2 * SLAB, 2 * SLAB)], sibling,
        )
    for w, (first, second) in enumerate(((at_x, at_y), (at_y, at_x))):
        for k, step, far in ((2, 1, 0), (1, -1, 1)):
            route(("r2", w, step, 0, far), tb(3, w, far * 64, 64), 64, second(step))
            for half in (0, 1):
                route(("r2", w, step, 1, half), tb(k, w, half * 64, 64), 64, second(step))
        for j, step, far in ((2, 1, 0), (1, -1, 1)):
            route(("r1", w, step, 0, far), tb(0, w, 3 * SUB + far * 16, 16), 16, first(step))
            for half in (0, 1):
                route(("r1", w, step, 1, half), tb(0, w, j * SUB + half * 16, 16), 16, first(step))

    barrier = pltpu.get_barrier_semaphore()
    for device in (at_z(1), at_z(-1), at_y(1), at_y(-1), at_x(1), at_x(-1), sibling):
        pl.semaphore_signal(barrier, inc=1, device_id=device, device_id_type=MESH_ID)

    s_all[pl.ds(OWN * NR, NR), :] = unit(audio_ref[...])[0].astype(BF16)
    t_unit = unit(text_ref[...])[0].astype(BF16)
    t_all[pl.ds(t_base(0, 0, 0), SUB), :] = t_unit[:SUB]
    t_all[pl.ds(t_base(0, 0, 1), SUB), :] = t_unit[SUB:]
    labels[pl.ds(OWN * 8, 8), :] = jnp.broadcast_to(label_ref[...], (8, NR))

    row = lax.broadcasted_iota(jnp.int32, ids.shape, 0)
    k, core, which, j, r = row >> 9, (row >> 8) & 1, (row >> 7) & 1, (row >> 5) & 3, row & 31

    def shift_of(slot):
        return jnp.where(slot == 1, 3, jnp.where(slot == 2, 1, jnp.where(slot == 3, 2, 0)))

    dk, dj = shift_of(k), shift_of(j)
    row_y = (y + jnp.where(which == 0, dk, dj)) & 3
    row_x = (x + jnp.where(which == 0, dj, dk)) & 3
    row_c = c ^ core
    ids[...] = zh * 4096 + row_y * 1024 + row_x * 256 + zl * 128 + row_c * 64 + which * 32 + r

    pl.semaphore_wait(barrier, 7)

    start(("s", L1, 0), ("s", R1, 1), ("t1", 0, 1), ("t1", 0, 2), ("t1", 1, 1), ("t1", 1, 2))
    start(("l", L1), ("l", R1), ("s", L1, 1), ("s", R1, 0))
    for w in (0, 1):
        start(("t2", w, 1, 0), ("t2", w, 2, 0))
    t_back[...] = jnp.zeros_like(t_back)
    s_back[...] = jnp.zeros_like(s_back)
    for w in (0, 1):
        wait(("t1", w, 1))
        start(("t1", w, 3, 0), ("t2", w, 1, 1), ("t2", w, 2, 1))
        wait(("t1", w, 2))
        start(("t1", w, 3, 1), ("t2", w, 1, 2), ("t2", w, 2, 2))
    wait(("s", L1, 0), ("s", R1, 1))
    start(("s", L2, 0), ("s", R2, 1))
    wait(("l", L1), ("l", R1))
    start(("l", L2), ("l", R2))
    for w in (0, 1):
        wait(("t1", w, 3, 0), ("t1", w, 3, 1))
        start(("t2", w, 1, 3), ("t2", w, 2, 3), ("ts", w, 0))
    for w in (0, 1):
        wait(("t2", w, 1, 0), ("t2", w, 1, 1))
        start(("t2", w, 3, 0))
    wait(("s", L1, 1), ("s", R1, 0))
    start(("s", L2, 1), ("s", R2, 0))
    wait(("ts", 0, 0), ("ts", 1, 0))

    def before_0():
        for w in (0, 1):
            wait(("t2", w, 2, 2), ("t2", w, 2, 3))
            start(("t2", w, 3, 1))
        for w in (0, 1):
            wait(("t2", w, 1, 2), ("t2", w, 1, 3))
            start(("ts", w, 1))
            wait(("t2", w, 2, 0), ("t2", w, 2, 1))
            start(("ts", w, 2))
        wait(("s", L2, 0), ("s", R2, 1), ("l", L2), ("l", R2))
        start(("s", L3, 0), ("s", R3, 1), ("l", L3), ("l", R3))
        wait(("ts", 0, 1), ("ts", 1, 1))

    def before_1():
        wait(("ts", 0, 2), ("ts", 1, 2))
        for w in (0, 1):
            wait(("t2", w, 3, 0), ("t2", w, 3, 1))
            start(("ts", w, 3))

    def before_2():
        wait(("s", L2, 1), ("s", R2, 0))
        start(("s", L3, 1), ("s", R3, 0))
        wait(("ts", 0, 3), ("ts", 1, 3))

    def before_4():
        wait(("s", L3, 0), ("s", R3, 1), ("l", L3), ("l", R3))
        start(("s", D4, 0), ("s", D4, 1), ("l", D4))

    def before_7():
        wait(("s", L3, 1), ("s", R3, 0))

    def before_11():
        wait(("s", D4, 0), ("s", D4, 1), ("l", D4))

    def before_12():
        for step, pieces in ((1, (2, 3)), (-1, (0, 1))):
            ship(*(("zr", step, 1, piece) for piece in pieces))

    def before_13():
        start(("sr", 3))

    before = {
        0: before_0, 1: before_1, 2: before_2, 4: before_4, 7: before_7, 11: before_11,
        12: before_12, 13: before_13,
    }

    sharp = sharp_ref[0]
    shift = shift_ref[0]

    def place(i):
        u = i // 4
        n = i % 4
        k = jnp.where(u == 3, jnp.where(n == 0, 3, jnp.where(n == 3, 0, n)), n)
        return pl.multiple_of(u * 256, 256), pl.multiple_of(k * CHUNK, CHUNK), pl.multiple_of(u * 16, 16)

    def forward(i, coefs):
        s0, t0, l0 = place(i)
        speech = s_all[pl.ds(s0, 256), :]
        lab_pair = labels[pl.ds(l0, 16), :]
        for half in range(2):
            rows = pl.ds(pl.multiple_of(t0 + half * 256, 256), 256)
            logits = lax.dot_general(
                t_all[rows, :], speech, (((1,), (1,)), ((), ())), preferred_element_type=F32
            )
            logits = sharp * logits + shift
            number = ids[rows, :]
            match = jnp.concatenate([number == lab_pair[0:1, :], number == lab_pair[8:9, :]], axis=1)
            coef = sharp * (1.0 / (1.0 + jnp.exp(-logits)) - match.astype(F32))
            coefs[pl.ds(half * 256, 256), :] = coef.astype(BF16)

    def backward(i, coefs):
        s0, t0, _ = place(i)
        coef = coefs[...]
        rows = pl.ds(t0, CHUNK)
        s_back[pl.ds(s0, 256), :] += lax.dot_general(
            coef, t_all[rows, :], (((0,), (0,)), ((), ())), preferred_element_type=F32
        )
        t_back[rows, :] += jnp.dot(coef, s_all[pl.ds(s0, 256), :], preferred_element_type=F32)

    forward(0, coef_even)

    def two_chunks(h, carry):
        for parity, ready, filled in ((0, coef_even, coef_odd), (1, coef_odd, coef_even)):
            for when, act in before.items():
                if when % 2 == parity:
                    pl.when(h == when // 2)(act)
            i = h * 2 + parity
            forward(i + 1, filled)
            backward(i, ready)
        return carry

    lax.fori_loop(0, 7, two_chunks, 0)

    def add(ref, other):
        ref[...] += other[...]

    def merge_sibling(k):
        wait(("sr", k))
        add(t_back.at[pl.ds(t_base(k, 0, 0), 2 * SLAB)], sib_back.at[pl.ds(k * 2 * SLAB, 2 * SLAB)])

    def z_step(order, pieces):
        for p in pieces:
            for step, chain in chains.items():
                piece = p if step == 1 else (p + 2) % 4
                ref = sb(chain[order + 1], piece)
                ref[...] += landed(("zr", step, order, piece))
                if order < 3:
                    ship(("zr", step, order + 1, piece))

    start(("sr", 1))
    forward(15, coef_odd)
    backward(14, coef_even)
    start(("sr", 2))
    merge_sibling(3)
    for w in (0, 1):
        ship(("r2", w, 1, 0, 0), ("r2", w, -1, 0, 1))
    backward(15, coef_odd)
    start(("sr", 0))
    ship(("zr", 1, 0, 0), ("zr", -1, 0, 2), ("zr", 1, 0, 1), ("zr", -1, 0, 3))
    merge_sibling(1)
    for w in (0, 1):
        ship(("r2", w, -1, 1, 0))
    merge_sibling(2)
    for w in (0, 1):
        ship(("r2", w, 1, 1, 1))
    z_step(1, (2, 3))
    z_step(0, (0, 1))
    for w in (0, 1):
        ref = tb(2, w, 0, 64)
        ref[...] += landed(("r2", w, 1, 0, 0))
        ship(("r2", w, 1, 1, 0))
        ref = tb(1, w, 64, 64)
        ref[...] += landed(("r2", w, -1, 0, 1))
        ship(("r2", w, -1, 1, 1))
    merge_sibling(0)
    z_step(2, (2, 3))
    z_step(1, (0, 1))
    for w in (0, 1):
        for half, step in ((1, 1), (0, -1), (0, 1), (1, -1)):
            ref = tb(0, w, half * 64, 64)
            ref[...] += landed(("r2", w, step, 1, half))
        ship(("r1", w, 1, 0, 0), ("r1", w, -1, 0, 1), ("r1", w, 1, 1, 1), ("r1", w, -1, 1, 0))
    z_step(2, (0, 1))
    for w in (0, 1):
        ref = tb(0, w, 2 * SUB, 16)
        ref[...] += landed(("r1", w, 1, 0, 0))
        ship(("r1", w, 1, 1, 0))
        ref = tb(0, w, SUB + 16, 16)
        ref[...] += landed(("r1", w, -1, 0, 1))
        ship(("r1", w, -1, 1, 1))
    z_step(3, (2, 3))
    for w in (0, 1):
        for half in (0, 1):
            ref = tb(0, w, half * 16, 16)
            ref[...] += landed(("r1", w, 1, 1, half)) + landed(("r1", w, -1, 1, half))
        rows = pl.ds(w * SUB, SUB)
        text_out[rows, :] = project(tb(0, w, 0, SUB)[...], text_ref[rows, :])
    z_step(3, (0, 1))
    speech_out[...] = project(s_back[pl.ds(OWN * NR, NR), :], audio_ref[...])

    for done in copies.values():
        done.wait_send()
    assert len(copies) == COPIES and len(routes) == ROUTES and used[0] == Q_ROWS


ROUTES = 28 + 12 + 12
Q_ROWS = 28 * PIECE + 12 * 64 + 12 * 16
COPIES = 14 + 7 + 2 * (4 + 8 + 2 + 4) + 4 + 2 * ROUTES


def shards(audio, sentence, matching, sharpness, offset):
    vmem = pl.BlockSpec(memory_space=pltpu.VMEM)
    smem = pl.BlockSpec(memory_space=pltpu.SMEM)
    return pl.pallas_call(
        kernel,
        out_shape=(jax.ShapeDtypeStruct((NR, E), F32), jax.ShapeDtypeStruct((NT, E), F32)),
        in_specs=[smem, smem, vmem, vmem, vmem],
        out_specs=(vmem, vmem),
        scratch_shapes=[
            pltpu.VMEM((8 * NR, E), BF16),
            pltpu.VMEM((4 * CHUNK, E), BF16),
            pltpu.VMEM((64, NR), jnp.int32),
            pltpu.VMEM((4 * CHUNK, 128), jnp.int32),
            pltpu.VMEM((4 * CHUNK, E), F32),
            pltpu.VMEM((8 * NR, E), F32),
            pltpu.VMEM((2 * CHUNK, E), F32),
            pltpu.VMEM((Q_ROWS, E), jnp.int16),
            pltpu.VMEM((Q_ROWS, E), jnp.int16),
            pltpu.VMEM((8 * ROUTES, 128), F32),
            pltpu.VMEM((8 * ROUTES, 128), F32),
            pltpu.VMEM((CHUNK, 256), BF16),
            pltpu.VMEM((CHUNK, 256), BF16),
            pltpu.SemaphoreType.DMA((COPIES,)),
            pltpu.SemaphoreType.DMA((COPIES,)),
        ],
        compiler_params=pltpu.CompilerParams(
            collective_id=0, has_side_effects=True, vmem_limit_bytes=60 * 1024 * 1024
        ),
    )(sharpness, offset, audio, sentence, matching.reshape(1, NR))


def solution(mesh):
    split = Mesh(mesh.devices.reshape(4, 4, 4, 2, 2), AXES)
    rows = P(AXES)
    return jax.shard_map(
        shards,
        mesh=split,
        in_specs=(rows, rows, rows, P(), P()),
        out_specs=(rows, rows),
        check_vma=False,
    )
```

```python
import functools

import jax
import jax.numpy as jnp
from jax import lax
from jax.experimental import pallas as pl
from jax.experimental.pallas import tpu as pltpu
from jax.sharding import Mesh
from jax.sharding import PartitionSpec as P

AXES = ("zh", "y", "x", "zl", "c")
MESH_ID = pl.DeviceIdType.MESH
F32 = jnp.float32
BF16 = jnp.bfloat16

L1, R1, L2, R2, L3, R3, OWN, D4 = range(8)
NR, NT, E = 128, 64, 768
HALF = NR // 2
PIECE = NR // 4
SLAB = 128
SUB = 32
CHUNK = 512


def unit(values):
    floats = values.astype(F32)
    norms = jnp.sqrt(jnp.sum(floats * floats, axis=-1, keepdims=True) + 1e-06)
    return floats / norms, norms


def project(back, values):
    direction, norms = unit(values)
    along = jnp.sum(direction * back, axis=-1, keepdims=True)
    return (back - direction * along) / norms


def kernel(
    sharp_ref, shift_ref, audio_ref, text_ref, label_ref,
    speech_out, text_out,
    s_all, t_all, labels, ids, t_back, s_back,
    sib_back, q_out, q_in, scale_out, scale_in,
    coef_even, coef_odd, send_sems, recv_sems,
):
    zh, y, x, zl, c = (lax.axis_index(a) for a in AXES)
    z = zh * 2 + zl

    def at_z(step):
        other = (z + step) % 8
        return (other // 2, y, x, other % 2, c)

    def at_y(step):
        return (zh, (y + step) % 4, x, zl, c)

    def at_x(step):
        return (zh, y, (x + step) % 4, zl, c)

    sibling = (zh, y, x, zl, 1 - c)
    copies = {}

    def copy(name, src, dst, device):
        q = len(copies)
        copies[name] = pltpu.make_async_remote_copy(
            src_ref=src, dst_ref=dst, send_sem=send_sems.at[q], recv_sem=recv_sems.at[q],
            device_id=device, device_id_type=MESH_ID,
        )

    def start(*names):
        for name in names:
            copies[name].start()

    def wait(*names):
        for name in names:
            copies[name].wait_recv()

    def s_rows(slot, half=None):
        if half is None:
            return s_all.at[pl.ds(slot * NR, NR)]
        return s_all.at[pl.ds(slot * NR + half * HALF, HALF)]

    def t_base(k, core, which):
        return k * CHUNK + core * 2 * SLAB + which * SLAB

    def t_rows(k, core, which, first, count):
        return t_all.at[pl.ds(t_base(k, core, which) + first, count)]

    def lab(slot):
        return labels.at[pl.ds(slot * 8, 8)]

    up = ((OWN, L1), (L1, L2), (L2, L3))
    down = ((OWN, R1), (R1, R2), (R2, R3))
    for pairs, step in ((up, 1), (down, -1)):
        for src, dst in pairs:
            for half in (0, 1):
                copy(("s", dst, half), s_rows(src, half), s_rows(dst, half), at_z(step))
            copy(("l", dst), lab(src), lab(dst), at_z(step))
    copy(("s", D4, 0), s_rows(L3, 0), s_rows(D4, 0), at_z(1))
    copy(("s", D4, 1), s_rows(R3, 1), s_rows(D4, 1), at_z(-1))
    copy(("l", D4), lab(L3), lab(D4), at_z(1))

    for w, (first, second) in enumerate(((at_x, at_y), (at_y, at_x))):
        piece = lambda j, lo=0, n=SUB: t_rows(0, 0, w, j * SUB + lo, n)
        for slot, step in ((1, 1), (2, -1), (3, 2)):
            copy(("t1", w, slot), piece(0), piece(slot), first(step))
            for j in range(4):
                copy(("t2", w, slot, j), piece(j), t_rows(slot, 0, w, j * SUB, SUB), second(step))
        for k in range(4):
            copy(("ts", w, k), t_rows(k, 0, w, 0, SLAB), t_rows(k, 1, w, 0, SLAB), sibling)

    routes = {}
    used = [0]

    def route(name, ref, rows, device):
        first, n = used[0], len(routes)
        used[0] += rows
        into = (q_in.at[pl.ds(first, rows)], scale_in.at[pl.ds(n * 8, 8)])
        out = (q_out.at[pl.ds(first, rows)], scale_out.at[pl.ds(n * 8, 8)])
        routes[name] = (ref, rows, out, into)
        for what, src, dst in zip("sq", reversed(out), reversed(into)):
            copy((*name, what), src, dst, device)

    def pack(name, value):
        _, rows, (numbers, scales), _ = routes[name]
        top = jnp.maximum(jnp.max(jnp.abs(value), axis=1, keepdims=True), 1e-30)
        numbers[...] = jnp.round(value * (32767.0 / top)).astype(jnp.int16)
        scale = top * (1.0 / 32767.0)
        lane = lax.broadcasted_iota(jnp.int32, (8, 128), 1)
        tile = jnp.zeros((8, 128), F32)
        for v in range(rows // 8):
            tile = jnp.where(lane == v, scale[v * 8 : v * 8 + 8], tile)
        scales[...] = tile

    def send(*names):
        for name in names:
            start((*name, "s"), (*name, "q"))

    def ship(*names):
        for name in names:
            pack(name, routes[name][0][...])
        send(*names)

    def arrived(*names):
        for name in names:
            wait((*name, "s"), (*name, "q"))

    def forward_sum(*pairs):
        arrived(*(come for come, _ in pairs))
        for come, leave in pairs:
            pack(leave, routes[leave][0][...] + unpacked(come))
        send(*(leave for _, leave in pairs))

    def unpacked(name):
        _, rows, _, (numbers, scales) = routes[name]
        tile = scales[...]
        scale = jnp.concatenate([tile[:, v : v + 1] for v in range(rows // 8)], axis=0)
        return numbers[...].astype(F32) * scale

    def sb(slot, piece):
        return s_back.at[pl.ds(slot * NR + piece * PIECE, PIECE)]

    chains = {1: (D4, R3, R2, R1, OWN), -1: (D4, L3, L2, L1, OWN)}
    far_pieces = {1: (0, 1), -1: (2, 3)}
    for step, chain in chains.items():
        for order, src in enumerate(chain[:-1]):
            for piece in range(4):
                if src != D4 or piece in far_pieces[step]:
                    route(("zr", step, order, piece), sb(src, piece), PIECE, at_z(step))

    def tb(k, which, first, count):
        return t_back.at[pl.ds(t_base(k, 0, which) + first, count)]

    for k in range(4):
        copy(
            ("sr", k), t_back.at[pl.ds(t_base(k, 1, 0), 2 * SLAB)],
            sib_back.at[pl.ds(k * 2 * SLAB, 2 * SLAB)], sibling,
        )
    for w, (first, second) in enumerate(((at_x, at_y), (at_y, at_x))):
        for slot, step in ((3, 2), (2, 1), (1, -1)):
            for half in (0, 1):
                route(("r2", w, slot, half), tb(slot, w, half * 64, 64), 64, second(step))
            route(("r1", w, slot), tb(0, w, slot * SUB, SUB), SUB, first(step))

    barrier = pltpu.get_barrier_semaphore()
    for device in (at_z(1), at_z(-1), at_y(1), at_y(-1), at_y(2), at_x(1), at_x(-1), at_x(2), sibling):
        pl.semaphore_signal(barrier, inc=1, device_id=device, device_id_type=MESH_ID)

    s_all[pl.ds(OWN * NR, NR), :] = unit(audio_ref[...])[0].astype(BF16)
    t_unit = unit(text_ref[...])[0].astype(BF16)
    t_all[pl.ds(t_base(0, 0, 0), SUB), :] = t_unit[:SUB]
    t_all[pl.ds(t_base(0, 0, 1), SUB), :] = t_unit[SUB:]
    labels[pl.ds(OWN * 8, 8), :] = jnp.broadcast_to(label_ref[...], (8, NR))

    row = lax.broadcasted_iota(jnp.int32, ids.shape, 0)
    k, core, which, j, r = row >> 9, (row >> 8) & 1, (row >> 7) & 1, (row >> 5) & 3, row & 31

    def shift_of(slot):
        return jnp.where(slot == 1, 3, jnp.where(slot == 2, 1, jnp.where(slot == 3, 2, 0)))

    dk, dj = shift_of(k), shift_of(j)
    row_y = (y + jnp.where(which == 0, dk, dj)) & 3
    row_x = (x + jnp.where(which == 0, dj, dk)) & 3
    row_c = c ^ core
    ids[...] = zh * 4096 + row_y * 1024 + row_x * 256 + zl * 128 + row_c * 64 + which * 32 + r

    pl.semaphore_wait(barrier, 9)

    start(("s", L1, 0), ("s", R1, 1))
    for slot in (1, 2, 3):
        start(("t1", 0, slot), ("t1", 1, slot))
    start(("l", L1), ("l", R1), ("s", L1, 1), ("s", R1, 0))
    for w in (0, 1):
        start(("t2", w, 1, 0), ("t2", w, 2, 0))
    t_back[...] = jnp.zeros_like(t_back)
    s_back[...] = jnp.zeros_like(s_back)
    for j in (1, 2):
        for w in (0, 1):
            wait(("t1", w, j))
            start(("t2", w, 1, j), ("t2", w, 2, j))
    wait(("s", L1, 0), ("s", R1, 1))
    start(("s", L2, 0), ("s", R2, 1))
    for w in (0, 1):
        wait(("t1", w, 3))
        start(("t2", w, 1, 3), ("t2", w, 2, 3), ("ts", w, 0))
    for w in (0, 1):
        start(*(("t2", w, 3, j) for j in range(4)))
    wait(("l", L1), ("l", R1))
    start(("l", L2), ("l", R2))
    wait(("s", L1, 1), ("s", R1, 0))
    start(("s", L2, 1), ("s", R2, 0))
    wait(("ts", 0, 0), ("ts", 1, 0))

    def before_0():
        for slot in (1, 2):
            for w in (0, 1):
                wait(*(("t2", w, slot, j) for j in range(4)))
                start(("ts", w, slot))
        wait(("s", L2, 0), ("s", R2, 1), ("l", L2), ("l", R2))
        start(("s", L3, 0), ("s", R3, 1), ("l", L3), ("l", R3))
        wait(("ts", 0, 1), ("ts", 1, 1))

    def before_1():
        wait(("ts", 0, 2), ("ts", 1, 2))

    def before_2():
        wait(("s", L2, 1), ("s", R2, 0))
        start(("s", L3, 1), ("s", R3, 0))

    def before_3():
        for w in (0, 1):
            wait(*(("t2", w, 3, j) for j in range(4)))
            start(("ts", w, 3))

    def before_4():
        wait(("s", L3, 0), ("s", R3, 1), ("l", L3), ("l", R3))
        start(("s", D4, 0), ("s", D4, 1), ("l", D4))

    def before_5():
        wait(("ts", 0, 3), ("ts", 1, 3))

    def before_7():
        wait(("s", L3, 1), ("s", R3, 0))

    def before_11():
        wait(("s", D4, 0), ("s", D4, 1), ("l", D4))

    def before_12():
        for step, pieces in ((1, (2, 3)), (-1, (0, 1))):
            ship(*(("zr", step, 1, piece) for piece in pieces))

    def before_13():
        start(("sr", 3))

    before = {
        0: before_0, 1: before_1, 2: before_2, 3: before_3, 4: before_4, 5: before_5, 7: before_7, 11: before_11,
        12: before_12, 13: before_13,
    }

    sharp = sharp_ref[0]
    shift = shift_ref[0]

    def place(i):
        n = i % 4
        u = jnp.where(i < 6, i // 3, jnp.where(i < 8, i - 6, i // 4))
        k = jnp.where(i < 6, i % 3, jnp.where(i < 8, 3, n))
        k = jnp.where(i < 12, k, jnp.where(n == 0, 3, jnp.where(n == 3, 0, n)))
        return pl.multiple_of(u * 256, 256), pl.multiple_of(k * CHUNK, CHUNK), pl.multiple_of(u * 16, 16)

    def forward(i, coefs):
        s0, t0, l0 = place(i)
        speech = s_all[pl.ds(s0, 256), :]
        lab_pair = labels[pl.ds(l0, 16), :]
        for half in range(2):
            rows = pl.ds(pl.multiple_of(t0 + half * 256, 256), 256)
            logits = lax.dot_general(
                t_all[rows, :], speech, (((1,), (1,)), ((), ())), preferred_element_type=F32
            )
            logits = sharp * logits + shift
            number = ids[rows, :]
            match = jnp.concatenate([number == lab_pair[0:1, :], number == lab_pair[8:9, :]], axis=1)
            coef = sharp * (1.0 / (1.0 + jnp.exp(-logits)) - match.astype(F32))
            coefs[pl.ds(half * 256, 256), :] = coef.astype(BF16)

    def backward(i, coefs):
        s0, t0, _ = place(i)
        coef = coefs[...]
        rows = pl.ds(t0, CHUNK)
        s_back[pl.ds(s0, 256), :] += lax.dot_general(
            coef, t_all[rows, :], (((0,), (0,)), ((), ())), preferred_element_type=F32
        )
        t_back[rows, :] += jnp.dot(coef, s_all[pl.ds(s0, 256), :], preferred_element_type=F32)

    forward(0, coef_even)

    def two_chunks(h, carry):
        for parity, ready, filled in ((0, coef_even, coef_odd), (1, coef_odd, coef_even)):
            for when, act in before.items():
                if when % 2 == parity:
                    pl.when(h == when // 2)(act)
            i = h * 2 + parity
            forward(i + 1, filled)
            backward(i, ready)
        return carry

    lax.fori_loop(0, 7, two_chunks, 0)

    def add(ref, other):
        ref[...] += other[...]

    def merge_sibling(k):
        wait(("sr", k))
        add(t_back.at[pl.ds(t_base(k, 0, 0), 2 * SLAB)], sib_back.at[pl.ds(k * 2 * SLAB, 2 * SLAB)])

    def z_step(order, *pieces):
        both = [(step, p if step == 1 else (p + 2) % 4) for p in pieces for step in (1, -1)]
        if order < 3:
            forward_sum(*((("zr", step, order, p), ("zr", step, order + 1, p)) for step, p in both))
            return
        for step, p in both:
            arrived(("zr", step, order, p))
            ref = sb(OWN, p)
            ref[...] += unpacked(("zr", step, order, p))

    def ship_slabs(k):
        merge_sibling(k)
        ship(*(("r2", w, k, half) for w in (0, 1) for half in (0, 1)))

    start(("sr", 1))
    forward(15, coef_odd)
    backward(14, coef_even)
    start(("sr", 2))
    backward(15, coef_odd)
    ship(("zr", 1, 0, 0), ("zr", -1, 0, 2))
    start(("sr", 0))
    ship(("zr", 1, 0, 1), ("zr", -1, 0, 3))
    ship_slabs(3)
    z_step(1, 2, 3)
    ship_slabs(1)
    ship_slabs(2)
    z_step(0, 0)
    z_step(0, 1)
    merge_sibling(0)
    z_step(2, 2, 3)
    z_step(1, 0)
    z_step(1, 1)
    for w in (0, 1):
        for half in (0, 1):
            for slot in (3, 1, 2):
                arrived(("r2", w, slot, half))
            ref = tb(0, w, half * 64, 64)
            ref[...] += unpacked(("r2", w, 3, half)) + unpacked(("r2", w, 1, half)) + unpacked(("r2", w, 2, half))
        ship(*(("r1", w, slot) for slot in (3, 2, 1)))
    z_step(3, 2, 3)
    z_step(2, 0)
    z_step(2, 1)
    for w in (0, 1):
        arrived(*(("r1", w, slot) for slot in (1, 2, 3)))
        back = tb(0, w, 0, SUB)[...] + unpacked(("r1", w, 1)) + unpacked(("r1", w, 2)) + unpacked(("r1", w, 3))
        rows = pl.ds(w * SUB, SUB)
        text_out[rows, :] = project(back, text_ref[rows, :])
    z_step(3, 0, 1)
    speech_out[...] = project(s_back[pl.ds(OWN * NR, NR), :], audio_ref[...])

    for done in copies.values():
        done.wait_send()
    assert len(copies) == COPIES and len(routes) == ROUTES and used[0] == Q_ROWS


ROUTES = 28 + 12 + 6
Q_ROWS = 28 * PIECE + 12 * 64 + 6 * SUB
COPIES = 14 + 7 + 2 * (3 + 12 + 4) + 4 + 2 * ROUTES


def shards(audio, sentence, matching, sharpness, offset):
    vmem = pl.BlockSpec(memory_space=pltpu.VMEM)
    smem = pl.BlockSpec(memory_space=pltpu.SMEM)
    return pl.pallas_call(
        kernel,
        out_shape=(jax.ShapeDtypeStruct((NR, E), F32), jax.ShapeDtypeStruct((NT, E), F32)),
        in_specs=[smem, smem, vmem, vmem, vmem],
        out_specs=(vmem, vmem),
        scratch_shapes=[
            pltpu.VMEM((8 * NR, E), BF16),
            pltpu.VMEM((4 * CHUNK, E), BF16),
            pltpu.VMEM((64, NR), jnp.int32),
            pltpu.VMEM((4 * CHUNK, 128), jnp.int32),
            pltpu.VMEM((4 * CHUNK, E), F32),
            pltpu.VMEM((8 * NR, E), F32),
            pltpu.VMEM((2 * CHUNK, E), F32),
            pltpu.VMEM((Q_ROWS, E), jnp.int16),
            pltpu.VMEM((Q_ROWS, E), jnp.int16),
            pltpu.VMEM((8 * ROUTES, 128), F32),
            pltpu.VMEM((8 * ROUTES, 128), F32),
            pltpu.VMEM((CHUNK, 256), BF16),
            pltpu.VMEM((CHUNK, 256), BF16),
            pltpu.SemaphoreType.DMA((COPIES,)),
            pltpu.SemaphoreType.DMA((COPIES,)),
        ],
        compiler_params=pltpu.CompilerParams(
            collective_id=0, has_side_effects=True, vmem_limit_bytes=60 * 1024 * 1024
        ),
    )(sharpness, offset, audio, sentence, matching.reshape(1, NR))


def solution(mesh):
    split = Mesh(mesh.devices.reshape(4, 4, 4, 2, 2), AXES)
    rows = P(AXES)
    return jax.shard_map(
        shards,
        mesh=split,
        in_specs=(rows, rows, rows, P(), P()),
        out_specs=(rows, rows),
        check_vma=False,
    )
```

```python
import functools

import jax
import jax.numpy as jnp
from jax import lax
from jax.experimental import pallas as pl
from jax.experimental.pallas import tpu as pltpu
from jax.sharding import Mesh
from jax.sharding import PartitionSpec as P

AXES = ("zh", "y", "x", "zl", "c")
MESH_ID = pl.DeviceIdType.MESH
F32 = jnp.float32
BF16 = jnp.bfloat16

L1, R1, L2, R2, L3, R3, OWN, D4 = range(8)
NR, NT, E = 128, 64, 768
HALF = NR // 2
PIECE = NR // 4
SLAB = 128
SUB = 32
CHUNK = 512


def unit(values):
    floats = values.astype(F32)
    norms = jnp.sqrt(jnp.sum(floats * floats, axis=-1, keepdims=True) + 1e-06)
    return floats / norms, norms


def project(back, values):
    direction, norms = unit(values)
    along = jnp.sum(direction * back, axis=-1, keepdims=True)
    return (back - direction * along) / norms


def kernel(
    sharp_ref, shift_ref, audio_ref, text_ref, label_ref,
    speech_out, text_out,
    s_all, t_all, labels, ids, t_back, s_back,
    sib_back, q_out, q_in, scale_out, scale_in,
    coef_even, coef_odd, send_sems, recv_sems,
):
    zh, y, x, zl, c = (lax.axis_index(a) for a in AXES)
    z = zh * 2 + zl

    def at_z(step):
        other = (z + step) % 8
        return (other // 2, y, x, other % 2, c)

    def at_y(step):
        return (zh, (y + step) % 4, x, zl, c)

    def at_x(step):
        return (zh, y, (x + step) % 4, zl, c)

    sibling = (zh, y, x, zl, 1 - c)
    copies = {}

    def copy(name, src, dst, device):
        q = len(copies)
        copies[name] = pltpu.make_async_remote_copy(
            src_ref=src, dst_ref=dst, send_sem=send_sems.at[q], recv_sem=recv_sems.at[q],
            device_id=device, device_id_type=MESH_ID,
        )

    def start(*names):
        for name in names:
            copies[name].start()

    def wait(*names):
        for name in names:
            copies[name].wait_recv()

    def s_rows(slot, half=None):
        if half is None:
            return s_all.at[pl.ds(slot * NR, NR)]
        return s_all.at[pl.ds(slot * NR + half * HALF, HALF)]

    def t_base(k, core, which):
        return k * CHUNK + core * 2 * SLAB + which * SLAB

    def t_rows(k, core, which, first, count):
        return t_all.at[pl.ds(t_base(k, core, which) + first, count)]

    def lab(slot):
        return labels.at[pl.ds(slot * 8, 8)]

    up = ((OWN, L1), (L1, L2), (L2, L3))
    down = ((OWN, R1), (R1, R2), (R2, R3))
    for pairs, step in ((up, 1), (down, -1)):
        for src, dst in pairs:
            for half in (0, 1):
                copy(("s", dst, half), s_rows(src, half), s_rows(dst, half), at_z(step))
            copy(("l", dst), lab(src), lab(dst), at_z(step))
    copy(("s", D4, 0), s_rows(L3, 0), s_rows(D4, 0), at_z(1))
    copy(("s", D4, 1), s_rows(R3, 1), s_rows(D4, 1), at_z(-1))
    copy(("l", D4), lab(L3), lab(D4), at_z(1))

    for w, (first, second) in enumerate(((at_x, at_y), (at_y, at_x))):
        piece = lambda j, lo=0, n=SUB: t_rows(0, 0, w, j * SUB + lo, n)
        for slot, step in ((1, 1), (2, -1), (3, 2)):
            copy(("t1", w, slot), piece(0), piece(slot), first(step))
            for j in range(4 if slot < 3 else 2):
                copy(("t2", w, slot, j), piece(j), t_rows(slot, 0, w, j * SUB, SUB), second(step))
        copy(("t2", w, 3, 2), t_rows(2, 0, w, 64, 64), t_rows(3, 0, w, 64, 64), second(-1))
        for k in range(4):
            copy(("ts", w, k), t_rows(k, 0, w, 0, SLAB), t_rows(k, 1, w, 0, SLAB), sibling)

    routes = {}
    used = [0]

    def route(name, ref, rows, device):
        first, n = used[0], len(routes)
        used[0] += rows
        into = (q_in.at[pl.ds(first, rows)], scale_in.at[pl.ds(n * 8, 8)])
        out = (q_out.at[pl.ds(first, rows)], scale_out.at[pl.ds(n * 8, 8)])
        routes[name] = (ref, rows, out, into)
        for what, src, dst in zip("sq", reversed(out), reversed(into)):
            copy((*name, what), src, dst, device)

    def pack(name, value):
        _, rows, (numbers, scales), _ = routes[name]
        top = jnp.maximum(jnp.max(jnp.abs(value), axis=1, keepdims=True), 1e-30)
        numbers[...] = jnp.round(value * (32767.0 / top)).astype(jnp.int16)
        scale = top * (1.0 / 32767.0)
        lane = lax.broadcasted_iota(jnp.int32, (8, 128), 1)
        tile = jnp.zeros((8, 128), F32)
        for v in range(rows // 8):
            tile = jnp.where(lane == v, scale[v * 8 : v * 8 + 8], tile)
        scales[...] = tile

    def send(*names):
        for name in names:
            start((*name, "s"), (*name, "q"))

    def ship(*names):
        for name in names:
            pack(name, routes[name][0][...])
        send(*names)

    def arrived(*names):
        for name in names:
            wait((*name, "s"), (*name, "q"))

    def forward_sum(*pairs):
        arrived(*(come for come, _ in pairs))
        for come, leave in pairs:
            pack(leave, routes[leave][0][...] + unpacked(come))
        send(*(leave for _, leave in pairs))

    def unpacked(name):
        _, rows, _, (numbers, scales) = routes[name]
        tile = scales[...]
        scale = jnp.concatenate([tile[:, v : v + 1] for v in range(rows // 8)], axis=0)
        return numbers[...].astype(F32) * scale

    def sb(slot, piece):
        return s_back.at[pl.ds(slot * NR + piece * PIECE, PIECE)]

    chains = {1: (D4, R3, R2, R1, OWN), -1: (D4, L3, L2, L1, OWN)}
    far_pieces = {1: (0, 1), -1: (2, 3)}
    for step, chain in chains.items():
        for order, src in enumerate(chain[:-1]):
            for piece in range(4):
                if src != D4 or piece in far_pieces[step]:
                    to = at_z(2 * step if src == D4 else step)
                    route(("zr", step, order, piece), sb(src, piece), PIECE, to)

    def tb(k, which, first, count):
        return t_back.at[pl.ds(t_base(k, 0, which) + first, count)]

    for k in range(4):
        copy(
            ("sr", k), t_back.at[pl.ds(t_base(k, 1, 0), 2 * SLAB)],
            sib_back.at[pl.ds(k * 2 * SLAB, 2 * SLAB)], sibling,
        )
    for w, (first, second) in enumerate(((at_x, at_y), (at_y, at_x))):
        for slot, step in ((3, 2), (2, 1), (1, -1)):
            for half in (0, 1):
                to = second(-1 if slot == 3 and half == 1 else step)
                route(("r2", w, slot, half), tb(slot, w, half * 64, 64), 64, to)
            route(("r1", w, slot), tb(0, w, slot * SUB, SUB), SUB, first(step))

    barrier = pltpu.get_barrier_semaphore()
    for device in (at_z(1), at_z(-1), at_z(2), at_z(-2), at_y(1), at_y(-1), at_y(2), at_x(1), at_x(-1), at_x(2), sibling):
        pl.semaphore_signal(barrier, inc=1, device_id=device, device_id_type=MESH_ID)

    s_all[pl.ds(OWN * NR, NR), :] = unit(audio_ref[...])[0].astype(BF16)
    t_unit = unit(text_ref[...])[0].astype(BF16)
    t_all[pl.ds(t_base(0, 0, 0), SUB), :] = t_unit[:SUB]
    t_all[pl.ds(t_base(0, 0, 1), SUB), :] = t_unit[SUB:]
    labels[pl.ds(OWN * 8, 8), :] = jnp.broadcast_to(label_ref[...], (8, NR))

    row = lax.broadcasted_iota(jnp.int32, ids.shape, 0)
    k, core, which, j, r = row >> 9, (row >> 8) & 1, (row >> 7) & 1, (row >> 5) & 3, row & 31

    def shift_of(slot):
        return jnp.where(slot == 1, 3, jnp.where(slot == 2, 1, jnp.where(slot == 3, 2, 0)))

    dk, dj = shift_of(k), shift_of(j)
    row_y = (y + jnp.where(which == 0, dk, dj)) & 3
    row_x = (x + jnp.where(which == 0, dj, dk)) & 3
    row_c = c ^ core
    ids[...] = zh * 4096 + row_y * 1024 + row_x * 256 + zl * 128 + row_c * 64 + which * 32 + r

    pl.semaphore_wait(barrier, 11)

    start(("s", L1, 0), ("s", R1, 1))
    for slot in (1, 2, 3):
        start(("t1", 0, slot), ("t1", 1, slot))
    start(("l", L1), ("l", R1), ("s", L1, 1), ("s", R1, 0))
    for w in (0, 1):
        start(("t2", w, 1, 0), ("t2", w, 2, 0))
    t_back[...] = jnp.zeros_like(t_back)
    s_back[...] = jnp.zeros_like(s_back)
    for j in (1, 2):
        for w in (0, 1):
            wait(("t1", w, j))
            start(("t2", w, 1, j), ("t2", w, 2, j))
    wait(("s", L1, 0), ("s", R1, 1))
    start(("s", L2, 0), ("s", R2, 1))
    for w in (0, 1):
        wait(("t1", w, 3))
        start(("t2", w, 1, 3), ("t2", w, 2, 3), ("ts", w, 0))
    for w in (0, 1):
        start(("t2", w, 3, 0), ("t2", w, 3, 1))
    wait(("l", L1), ("l", R1))
    start(("l", L2), ("l", R2))
    wait(("s", L1, 1), ("s", R1, 0))
    start(("s", L2, 1), ("s", R2, 0))
    wait(("ts", 0, 0), ("ts", 1, 0))

    def before_0():
        for w in (0, 1):
            wait(("t2", w, 2, 2), ("t2", w, 2, 3))
            start(("t2", w, 3, 2))
        for slot in (1, 2):
            for w in (0, 1):
                wait(*(("t2", w, slot, j) for j in range(4 if slot == 1 else 2)))
                start(("ts", w, slot))
        wait(("s", L2, 0), ("s", R2, 1), ("l", L2), ("l", R2))
        start(("s", L3, 0), ("s", R3, 1), ("l", L3), ("l", R3))
        wait(("ts", 0, 1), ("ts", 1, 1))

    def before_1():
        wait(("ts", 0, 2), ("ts", 1, 2))

    def before_2():
        wait(("s", L2, 1), ("s", R2, 0))
        start(("s", L3, 1), ("s", R3, 0))

    def before_3():
        for w in (0, 1):
            wait(*(("t2", w, 3, j) for j in range(3)))
            start(("ts", w, 3))

    def before_4():
        wait(("s", L3, 0), ("s", R3, 1), ("l", L3), ("l", R3))
        start(("s", D4, 0), ("s", D4, 1), ("l", D4))

    def before_5():
        wait(("ts", 0, 3), ("ts", 1, 3))

    def before_7():
        wait(("s", L3, 1), ("s", R3, 0))

    def before_11():
        wait(("s", D4, 0), ("s", D4, 1), ("l", D4))

    def before_12():
        for pieces in ((2, 3), (0, 1)):
            ship(*(("zr", step, 1, p if step == 1 else (p + 2) % 4) for p in pieces for step in (1, -1)))

    def before_13():
        start(("sr", 3))

    before = {
        0: before_0, 1: before_1, 2: before_2, 3: before_3, 4: before_4, 5: before_5, 7: before_7, 11: before_11,
        12: before_12, 13: before_13,
    }

    sharp = sharp_ref[0]
    shift = shift_ref[0]

    def place(i):
        n = i % 4
        u = jnp.where(i < 6, i // 3, jnp.where(i < 8, i - 6, i // 4))
        k = jnp.where(i < 6, i % 3, jnp.where(i < 8, 3, n))
        k = jnp.where(i < 12, k, jnp.where(n == 0, 3, jnp.where(n == 3, 0, n)))
        return pl.multiple_of(u * 256, 256), pl.multiple_of(k * CHUNK, CHUNK), pl.multiple_of(u * 16, 16)

    def forward(i, coefs):
        s0, t0, l0 = place(i)
        speech = s_all[pl.ds(s0, 256), :]
        lab_pair = labels[pl.ds(l0, 16), :]
        for half in range(2):
            rows = pl.ds(pl.multiple_of(t0 + half * 256, 256), 256)
            logits = lax.dot_general(
                t_all[rows, :], speech, (((1,), (1,)), ((), ())), preferred_element_type=F32
            )
            logits = sharp * logits + shift
            number = ids[rows, :]
            match = jnp.concatenate([number == lab_pair[0:1, :], number == lab_pair[8:9, :]], axis=1)
            coef = sharp * (1.0 / (1.0 + jnp.exp(-logits)) - match.astype(F32))
            coefs[pl.ds(half * 256, 256), :] = coef.astype(BF16)

    def backward(i, coefs):
        s0, t0, _ = place(i)
        coef = coefs[...]
        rows = pl.ds(t0, CHUNK)
        s_back[pl.ds(s0, 256), :] += lax.dot_general(
            coef, t_all[rows, :], (((0,), (0,)), ((), ())), preferred_element_type=F32
        )
        t_back[rows, :] += jnp.dot(coef, s_all[pl.ds(s0, 256), :], preferred_element_type=F32)

    forward(0, coef_even)

    def two_chunks(h, carry):
        for parity, ready, filled in ((0, coef_even, coef_odd), (1, coef_odd, coef_even)):
            for when, act in before.items():
                if when % 2 == parity:
                    pl.when(h == when // 2)(act)
            i = h * 2 + parity
            forward(i + 1, filled)
            backward(i, ready)
        return carry

    lax.fori_loop(0, 7, two_chunks, 0)

    def add(ref, other):
        ref[...] += other[...]

    def merge_sibling(k):
        wait(("sr", k))
        add(t_back.at[pl.ds(t_base(k, 0, 0), 2 * SLAB)], sib_back.at[pl.ds(k * 2 * SLAB, 2 * SLAB)])

    def z_step(order, *pieces):
        both = [(step, p if step == 1 else (p + 2) % 4) for p in pieces for step in (1, -1)]
        if order < 3:
            forward_sum(*((("zr", step, order, p), ("zr", step, order + 1, p)) for step, p in both))
            return
        for step, p in both:
            arrived(("zr", step, order, p))
            ref = sb(OWN, p)
            ref[...] += unpacked(("zr", step, order, p))

    def z_far(piece):
        both = [(step, piece if step == 1 else (piece + 2) % 4) for step in (1, -1)]
        for step, p in both:
            arrived(("zr", step, 0, p), ("zr", step, 1, p))
        for step, p in both:
            leave = ("zr", step, 2, p)
            pack(leave, routes[leave][0][...] + unpacked(("zr", step, 1, p)) + unpacked(("zr", step, 0, p)))
        send(*(("zr", step, 2, p) for step, p in both))

    def ship_slabs(k, halves):
        merge_sibling(k)
        ship(*(("r2", w, k, half) for w in (0, 1) for half in halves))

    start(("sr", 1))
    forward(15, coef_odd)
    backward(14, coef_even)
    start(("sr", 2))
    backward(15, coef_odd)
    start(("sr", 0))
    ship(("zr", 1, 0, 0), ("zr", -1, 0, 2))
    ship(("zr", 1, 0, 1), ("zr", -1, 0, 3))
    ship_slabs(3, (1, 0))
    z_step(1, 2, 3)
    ship_slabs(1, (0,))
    ship_slabs(2, (0, 1))
    z_far(0)
    z_far(1)
    forward_sum(*((("r2", w, 3, 1), ("r2", w, 1, 1)) for w in (0, 1)))
    z_step(2, 2, 3)
    merge_sibling(0)
    z_step(2, 0)
    z_step(2, 1)
    for half, slots in ((0, (1, 3, 2)), (1, (2, 1))):
        for w in (0, 1):
            arrived(*(("r2", w, slot, half) for slot in slots))
            ref = tb(0, w, half * 64, 64)
            ref[...] += sum(unpacked(("r2", w, slot, half)) for slot in slots)
    for w in (0, 1):
        ship(*(("r1", w, slot) for slot in (3, 2, 1)))
    z_step(3, 2, 3)
    z_step(3, 0, 1)
    speech_out[...] = project(s_back[pl.ds(OWN * NR, NR), :], audio_ref[...])
    for w in (0, 1):
        arrived(*(("r1", w, slot) for slot in (1, 2, 3)))
        back = tb(0, w, 0, SUB)[...] + unpacked(("r1", w, 1)) + unpacked(("r1", w, 2)) + unpacked(("r1", w, 3))
        rows = pl.ds(w * SUB, SUB)
        text_out[rows, :] = project(back, text_ref[rows, :])

    for done in copies.values():
        done.wait_send()
    assert len(copies) == COPIES and len(routes) == ROUTES and used[0] == Q_ROWS


ROUTES = 28 + 12 + 6
Q_ROWS = 28 * PIECE + 12 * 64 + 6 * SUB
COPIES = 14 + 7 + 2 * (3 + 11 + 4) + 4 + 2 * ROUTES


def shards(audio, sentence, matching, sharpness, offset):
    vmem = pl.BlockSpec(memory_space=pltpu.VMEM)
    smem = pl.BlockSpec(memory_space=pltpu.SMEM)
    return pl.pallas_call(
        kernel,
        out_shape=(jax.ShapeDtypeStruct((NR, E), F32), jax.ShapeDtypeStruct((NT, E), F32)),
        in_specs=[smem, smem, vmem, vmem, vmem],
        out_specs=(vmem, vmem),
        scratch_shapes=[
            pltpu.VMEM((8 * NR, E), BF16),
            pltpu.VMEM((4 * CHUNK, E), BF16),
            pltpu.VMEM((64, NR), jnp.int32),
            pltpu.VMEM((4 * CHUNK, 128), jnp.int32),
            pltpu.VMEM((4 * CHUNK, E), F32),
            pltpu.VMEM((8 * NR, E), F32),
            pltpu.VMEM((2 * CHUNK, E), F32),
            pltpu.VMEM((Q_ROWS, E), jnp.int16),
            pltpu.VMEM((Q_ROWS, E), jnp.int16),
            pltpu.VMEM((8 * ROUTES, 128), F32),
            pltpu.VMEM((8 * ROUTES, 128), F32),
            pltpu.VMEM((CHUNK, 256), BF16),
            pltpu.VMEM((CHUNK, 256), BF16),
            pltpu.SemaphoreType.DMA((COPIES,)),
            pltpu.SemaphoreType.DMA((COPIES,)),
        ],
        compiler_params=pltpu.CompilerParams(
            collective_id=0, has_side_effects=True, vmem_limit_bytes=60 * 1024 * 1024
        ),
    )(sharpness, offset, audio, sentence, matching.reshape(1, NR))


def solution(mesh):
    split = Mesh(mesh.devices.reshape(4, 4, 4, 2, 2), AXES)
    rows = P(AXES)
    return jax.shard_map(
        shards,
        mesh=split,
        in_specs=(rows, rows, rows, P(), P()),
        out_specs=(rows, rows),
        check_vma=False,
    )
```
